32 devices in a mesh: head: 4 (over x, core), seq: 8 (over z, y).
Axes of the slice: x: 2, y: 2, z: 4, core: 2. Of those that a mesh axis runs over, the one named last changes fastest.
Arguments:
- skip_stream: bfloat16 [4096, 1024], P('head', 'seq'), may hold values from -6 to 6
- acceptance_vector: bfloat16 [4096, 1024], P('head', 'seq'), may hold values from -6 to 6
- address_vectors: bfloat16 [4096, 1024], P('head', 'seq'), may hold values from -0.75 to 0.75
- content_vectors: bfloat16 [4096, 1024], P('head', 'seq'), may hold values from -6 to 6
- emission_valve: bfloat16 [4096, 1024], P('head', 'seq'), may hold values from -6 to 6
- fading_exponent: bfloat16 [4096, 1024], P('head', 'seq'), may hold values from -0.7 to 0
- adaptation_speed: bfloat16 [4096, 1024], P('head', 'seq'), may hold values from 0 to 0.9
- erasure_factor: float32 [4096], P('head'), may hold values from 0.3 to 3
- reward_coefficient: float32 [4096], P('head'), may hold values from -4 to 4
- cluster_multiplier: float32 [4096], P('head'), may hold values from 0.5 to 2
- cluster_offset: float32 [4096], P('head'), may hold values from -3 to 3
- projection_weights: bfloat16 [4096, 4096], P(None, 'head'), may hold values from -0.125 to 0.125
Outputs:
- layer_output: bfloat16 [4096, 1024], P('head', 'seq')
The draws below stay inside these ranges and needn't reach their ends.
All inputs are finite; a program needn't handle non-finite values.
Results may differ from the reference program's by a relative error of at most 0.0048.
Values may be sent and summed in bfloat16 or wider, within the bound.
A program may use at most 128 MiB of HBM per device.

```python
import math
import jax
import jax.numpy as jnp
from jax import lax

EMBED_DIMENSION = 4096
ATTENTION_UNITS = 64
UNIT_CHANNELS = 64
TOK_DEV = 128
TOKEN_COUNT = 1024


def head_classes(key):
    order = jax.random.permutation(jax.random.fold_in(key, 101), ATTENTION_UNITS)
    fast_count = ATTENTION_UNITS // 2
    return order >= fast_count


def unit_ranks(key):
    unit_keys = jax.random.split(jax.random.fold_in(key, 107), ATTENTION_UNITS)
    return jax.vmap(lambda unit_key: jax.random.permutation(unit_key, UNIT_CHANNELS))(unit_keys)


def long_channels(key):
    return unit_ranks(key) >= UNIT_CHANNELS - UNIT_CHANNELS // 4


def quick_channels(key):
    ranks = unit_ranks(key)
    return jnp.logical_and(ranks >= UNIT_CHANNELS // 4, ranks < UNIT_CHANNELS // 2)


def steady_places(key):
    chosen = unit_ranks(key) < UNIT_CHANNELS // 4
    slab_count = TOKEN_COUNT // TOK_DEV
    slab_pick = jax.random.randint(jax.random.fold_in(key, 108), (ATTENTION_UNITS, UNIT_CHANNELS, slab_count), 0, 4) == 0
    slab_pick = jnp.repeat(slab_pick, TOK_DEV, axis=2)
    return jnp.logical_and(chosen[:, :, None], slab_pick)


def draw_fading_exponent(key, part):
    slow_heads = head_classes(key)
    keeps_long = jnp.logical_or(slow_heads[:, None], long_channels(key))
    factor = jnp.exp(jax.random.uniform(jax.random.fold_in(key, 102), (ATTENTION_UNITS, UNIT_CHANNELS, TOKEN_COUNT), jnp.float32, -math.log(2.0), math.log(2.0)))
    sequential_field = -0.4 / TOKEN_COUNT * factor
    fast_field = -2.3 / 40.0 * factor
    places = jax.random.randint(jax.random.fold_in(key, 103), (2,), 0, TOKEN_COUNT)
    removed_state = jnp.any(jnp.arange(TOKEN_COUNT)[:, None] == places[None, :], axis=1)
    block_outputs = jnp.log(jax.random.uniform(jax.random.fold_in(key, 104), (ATTENTION_UNITS, UNIT_CHANNELS, TOKEN_COUNT), jnp.float32, 0.5, 0.8))
    sequential_field = jnp.where(removed_state[None, None, :], block_outputs, sequential_field)
    field = jnp.where(keeps_long[:, :, None], sequential_field, fast_field)
    steady_field = jax.random.uniform(jax.random.fold_in(key, 109), (ATTENTION_UNITS, UNIT_CHANNELS, TOKEN_COUNT), jnp.float32, -0.7, -0.69)
    field = jnp.where(steady_places(key), steady_field, field)
    return field.reshape(EMBED_DIMENSION, TOKEN_COUNT).astype(jnp.bfloat16)


def draw_adaptation_speed(key, part):
    slow_heads = head_classes(key)
    slow_rate = jnp.where(slow_heads[:, None], jnp.logical_not(quick_channels(key)), long_channels(key))
    factor = jnp.exp(jax.random.uniform(jax.random.fold_in(key, 105), (ATTENTION_UNITS, UNIT_CHANNELS, TOKEN_COUNT), jnp.float32, -math.log(2.0), math.log(2.0)))
    sequential_field = 32.0 / TOKEN_COUNT * factor
    fast_field = jnp.exp(jax.random.uniform(jax.random.fold_in(key, 106), (ATTENTION_UNITS, UNIT_CHANNELS, TOKEN_COUNT), jnp.float32, math.log(0.05), math.log(0.9)))
    quick_field = jnp.exp(jax.random.uniform(jax.random.fold_in(key, 110), (ATTENTION_UNITS, UNIT_CHANNELS, TOKEN_COUNT), jnp.float32, math.log(0.2), math.log(0.9)))
    rapid_field = jnp.where(slow_heads[:, None, None], quick_field, fast_field)
    field = jnp.where(slow_rate[:, :, None], sequential_field, rapid_field)
    return field.reshape(EMBED_DIMENSION, TOKEN_COUNT).astype(jnp.bfloat16)


def strengthened(entries, key, source, target, parts, factor):
    owner, partner = [(jnp.arange(entries.shape[dim]) // (entries.shape[dim] // parts)).reshape([-1 if axis == dim else 1 for axis in range(entries.ndim)]) for dim in (source, target)]
    chosen = jax.random.permutation(key, parts)[partner]
    strong = (owner == chosen) | (owner == (partner + parts // 2) % parts)
    return jnp.where(strong, factor * entries, entries)


def shard_levels(stream_key, shape, shards, low, top_value):
    def one(position, parts):
        steps = jax.random.uniform(jax.random.fold_in(jax.random.fold_in(stream_key, 6), position), (parts,), jnp.float32, low / len(shards), top_value / len(shards))
        return jnp.repeat(jnp.exp(steps), shape[position] // parts).reshape((-1,) + (1,) * (len(shape) - position - 1))

    gain = one(*shards[0])
    for cut in shards[1:]:
        gain = gain * one(*cut)
    return gain


def bell_draw(key, dims, scale, most, cuts=(), kind=jnp.bfloat16):
    values = scale * jax.random.normal(key, dims, jnp.float32)
    if cuts:
        values = values * shard_levels(key, dims, cuts, -0.22, 0.18)
    return jnp.clip(values, -most, most).astype(kind)


def heavy_noise(stream_key, dims, width, bound, pieces, heavy, kind=jnp.bfloat16):
    values = width * jax.random.normal(stream_key, dims, jnp.float32)
    if pieces:
        values = values * shard_levels(stream_key, dims, pieces, -0.22, 0.18)
    return jnp.clip(strengthened(values, jax.random.fold_in(stream_key, 3), *heavy), -bound, bound).astype(kind)


def setup_inputs(seed: int = 0) -> dict:
    key_of = jax.random.split(jax.random.key(seed), 13)
    skip_stream = bell_draw(key_of[0], (EMBED_DIMENSION, TOKEN_COUNT), 1.0, 6.0, ((0, 4), (1, 8)))
    acceptance_vector = bell_draw(key_of[1], (EMBED_DIMENSION, TOKEN_COUNT), 1.0, 6.0, ((0, 4), (1, 8)))
    address_vectors = bell_draw(key_of[2], (EMBED_DIMENSION, TOKEN_COUNT), 0.125, 0.75, ((0, 4), (1, 8)))
    content_vectors = bell_draw(key_of[3], (EMBED_DIMENSION, TOKEN_COUNT), 1.0, 6.0, ((0, 4), (1, 8)))
    emission_valve = bell_draw(key_of[4], (EMBED_DIMENSION, TOKEN_COUNT), 1.0, 6.0, ((0, 4), (1, 8)))
    fading_exponent = draw_fading_exponent(jax.random.fold_in(key_of[12], 71), 0)
    adaptation_speed = draw_adaptation_speed(jax.random.fold_in(key_of[12], 71), 0)
    erasure_factor = jnp.clip(jnp.exp(math.log(3.0) - 2.3025851 * jax.random.uniform(key_of[7], (EMBED_DIMENSION,), jnp.float32) ** shard_levels(key_of[7], (EMBED_DIMENSION,), ((0, 4),), -0.2, 0.2)), 0.3, 3.0)
    reward_coefficient = bell_draw(key_of[8], (EMBED_DIMENSION,), 1.0, 4.0, ((0, 4),), jnp.float32)
    cluster_multiplier = jnp.clip(jnp.exp(math.log(2.0) - 1.3862944 * jax.random.uniform(key_of[9], (EMBED_DIMENSION,), jnp.float32) ** shard_levels(key_of[9], (EMBED_DIMENSION,), ((0, 4),), -0.2, 0.2)), 0.5, 2.0)
    cluster_offset = bell_draw(key_of[10], (EMBED_DIMENSION,), 0.5, 3.0, ((0, 4),), jnp.float32)
    projection_weights = heavy_noise(key_of[11], (EMBED_DIMENSION, EMBED_DIMENSION), EMBED_DIMENSION ** -0.5, 0.125, ((1, 4),), (1, 0, 4, 2.0))
    return {"skip_stream": skip_stream, "acceptance_vector": acceptance_vector, "address_vectors": address_vectors, "content_vectors": content_vectors, "emission_valve": emission_valve, "fading_exponent": fading_exponent, "adaptation_speed": adaptation_speed, "erasure_factor": erasure_factor, "reward_coefficient": reward_coefficient, "cluster_multiplier": cluster_multiplier, "cluster_offset": cluster_offset, "projection_weights": projection_weights}


HIGHEST = lax.Precision.HIGHEST

def position_results(field):
    return jnp.transpose(field.astype(jnp.float32).reshape(ATTENTION_UNITS, UNIT_CHANNELS, TOK_DEV), (2, 0, 1))

def as_blocks(field):
    return jnp.transpose(field.reshape(field.shape[0], TOKEN_COUNT // TOK_DEV, TOK_DEV), (1, 0, 2))

def wkv_step(memory, token_item):
    recept_now, key_now, value_now, decay_now, removal_now, rate_now = token_item
    removed = jnp.einsum('hvk,hk->hv', memory, removal_now, precision=HIGHEST)
    memory = memory * jnp.exp(decay_now)[:, None, :] - removed[:, :, None] * (removal_now * rate_now)[:, None, :] + value_now[:, :, None] * key_now[:, None, :]
    return (memory, jnp.einsum('hvk,hk->hv', memory, recept_now, precision=HIGHEST))

def reference(skip_stream, acceptance_vector, address_vectors, content_vectors, emission_valve, fading_exponent, adaptation_speed, erasure_factor, reward_coefficient, cluster_multiplier, cluster_offset, projection_weights):
    scale_heads = erasure_factor.reshape(ATTENTION_UNITS, UNIT_CHANNELS)
    reward_each_unit = reward_coefficient.reshape(ATTENTION_UNITS, UNIT_CHANNELS)
    gain_heads = cluster_multiplier.reshape(ATTENTION_UNITS, UNIT_CHANNELS)
    bias_heads = cluster_offset.reshape(ATTENTION_UNITS, UNIT_CHANNELS)

    def run_block(memory, block_item):
        recept_part, key_part, value_part, valve_portion, decay_part, rate_part = block_item
        acceptance_column = position_results(recept_part)
        address_column = position_results(key_part)
        content_column = position_results(value_part)
        decay_tok = position_results(decay_part)
        rate_tok = position_results(rate_part)
        scaled = address_column * scale_heads
        removal = scaled * lax.rsqrt(lax.optimization_barrier(jnp.sum(scaled * scaled, axis=2, keepdims=True)) + 1e-06)
        memory, read_out = lax.scan(wkv_step, memory, (acceptance_column, address_column, content_column, decay_tok, removal, rate_tok))
        centre = lax.optimization_barrier(jnp.mean(read_out, axis=2, keepdims=True))
        centred = read_out - centre
        spread = lax.optimization_barrier(jnp.mean(centred * centred, axis=2, keepdims=True))
        standardised = centred * lax.rsqrt(spread + 0.00064) * gain_heads + bias_heads
        reward_addend = lax.optimization_barrier(jnp.sum(acceptance_column * address_column * reward_each_unit, axis=2, keepdims=True)) * content_column
        blended_content = (standardised + reward_addend) * position_results(valve_portion)
        blended_content = jnp.transpose(blended_content, (1, 2, 0)).reshape(EMBED_DIMENSION, TOK_DEV).astype(jnp.bfloat16)
        return (memory, blended_content)
    start = jnp.zeros((ATTENTION_UNITS, UNIT_CHANNELS, UNIT_CHANNELS), jnp.float32)
    final_memory, mixed_blocks = lax.scan(run_block, start, (as_blocks(acceptance_vector), as_blocks(address_vectors), as_blocks(content_vectors), as_blocks(emission_valve), as_blocks(fading_exponent), as_blocks(adaptation_speed)))
    blended_content = jnp.transpose(mixed_blocks, (1, 0, 2)).reshape(EMBED_DIMENSION, TOKEN_COUNT)
    projected = jnp.dot(projection_weights, blended_content, preferred_element_type=jnp.float32)
    return (projected + skip_stream.astype(jnp.float32)).astype(jnp.bfloat16)
```

```python
import functools

import jax
import jax.numpy as jnp
from jax import lax
from jax.experimental import pallas as pl
from jax.experimental.pallas import tpu as pltpu
from jax.sharding import PartitionSpec as P

MESH = pl.DeviceIdType.MESH
UNIT = 64
GROUP = 4
F32 = jnp.float32
BF16 = jnp.bfloat16


def split(x):
    hi = x.astype(BF16)
    return hi, (x - hi.astype(F32)).astype(BF16)


def mm(a, b, ca=1, cb=0, passes=3):
    dims = (((ca,), (cb,)), ((), ()))
    if passes == 1:
        return lax.dot_general(a.astype(BF16), b.astype(BF16), dims, preferred_element_type=F32)
    if a.dtype == BF16:
        bh, bl = split(b)
        a2 = jnp.concatenate([a, a], axis=ca)
        b2 = jnp.concatenate([bh, bl], axis=cb)
        return lax.dot_general(a2, b2, dims, preferred_element_type=F32)
    ah, al = split(a)
    bh, bl = split(b)
    a3 = jnp.concatenate([ah, ah, al], axis=ca)
    b3 = jnp.concatenate([bh, bl, bh], axis=cb)
    return lax.dot_general(a3, b3, dims, preferred_element_type=F32)


def columns_of(row_ref, first, count):
    i = lax.broadcasted_iota(jnp.int32, (128, 128), 0)
    j = lax.broadcasted_iota(jnp.int32, (128, 128), 1)
    eye = i == j
    out = []
    for n in range(count):
        row = row_ref[pl.ds(first + n, 1), :]
        out.append(jnp.sum(jnp.where(eye, jnp.broadcast_to(row, (128, 128)), 0.0), axis=1, keepdims=True))
    return jnp.concatenate(out, axis=0) if count > 1 else out[0]


def local_kernel(r_ref, k_ref, v_ref, w_ref, a_ref, er_ref, tp_ref, loc_ref, st_ref):
    length = r_ref.shape[1]
    mid_at = length // 2 - 1
    si = lax.broadcasted_iota(jnp.int32, (length, length), 0)
    ti = lax.broadcasted_iota(jnp.int32, (length, length), 1)
    ones = jnp.where(si <= ti, 1.0, 0.0) - jnp.where(si <= mid_at, 1.0, 0.0)
    w16 = w_ref[...]
    c = jnp.dot(w16, ones.astype(BF16), preferred_element_type=F32)
    w = w16.astype(F32)
    er = columns_of(er_ref, pl.program_id(0) * (GROUP // 2), GROUP // 2)
    k = k_ref[...].astype(F32)
    scaled = k * er
    heads = range(GROUP)
    sl = [slice(h * UNIT, (h + 1) * UNIT) for h in heads]
    kk = jnp.concatenate(
        [scaled[s] * lax.rsqrt(jnp.sum(scaled[s] * scaled[s], axis=0, keepdims=True) + 1e-06) for s in sl], axis=0
    )
    back = jnp.exp(-c)
    pulled_back = a_ref[...].astype(F32) * kk * back
    keys_back = k * back
    removal = -kk * jnp.exp(c - w)
    recept = r_ref[...].astype(F32) * jnp.exp(c)
    emid = jnp.exp(w[:, 0:1] - c[:, 0:1])
    eend = jnp.exp(c[:, length - 1 :])
    etot = emid * eend
    pulled_end = pulled_back * eend
    keys_end = keys_back * eend

    before = si < ti
    upto = si <= ti
    mix = [
        mm(
            jnp.concatenate([pulled_back[s], keys_back[s]], axis=1),
            jnp.concatenate([removal[s], recept[s]], axis=1),
            0,
            0,
        )
        for s in sl
    ]
    pair_mix = [jnp.where(before, m[:length, :length], 0.0) for m in mix]
    key_mix = [jnp.where(before, m[length:, :length], 0.0) for m in mix]
    pair_read = [jnp.where(upto, m[:length, length:], 0.0) for m in mix]
    key_read = [jnp.where(upto, m[length:, length:], 0.0) for m in mix]
    eye = jnp.where(si == ti, 1.0, 0.0)
    size = 1
    inv = None
    while size < length:
        joins = (si // (2 * size) == ti // (2 * size)) & (si // size != ti // size)
        off = [jnp.where(joins, m, 0.0) for m in pair_mix]
        if inv is None:
            inv = [eye + o for o in off]
        else:
            half = [mm(n, o) for n, o in zip(inv, off)]
            inv = [n + mm(x, n) for n, x in zip(inv, half)]
        size *= 2
    v16 = v_ref[...]
    vk = [mm(v16[s], m) for s, m in zip(sl, key_mix)]
    solved = [mm(jnp.concatenate([x, removal[s]], axis=0), n) for x, s, n in zip(vk, sl, inv)]
    solved = [jnp.concatenate([x[:UNIT], x[UNIT:] * emid[s]], axis=0) for x, s in zip(solved, sl)]
    ends = [mm(x, pulled_end[s], 1, 1) for x, s in zip(solved, sl)]
    vke = [mm(v16[s], keys_end[s], 1, 1) for s in sl]
    reads = [mm(x, p) for x, p in zip(solved, pair_read)]
    vkr = [mm(v16[s], m) for s, m in zip(sl, key_read)]
    diag = lax.broadcasted_iota(jnp.int32, (UNIT, UNIT), 0) == lax.broadcasted_iota(jnp.int32, (UNIT, UNIT), 1)
    for h in heads:
        s = sl[h]
        trans = ends[h][UNIT:] + jnp.where(diag, jnp.broadcast_to(etot[s], (UNIT, UNIT)), 0.0)
        tp_ref[s, :] = jnp.concatenate([trans, ends[h][:UNIT] + vke[h]], axis=1)
        loc_ref[s, :] = reads[h][:UNIT] + vkr[h]
        st_ref[s, :] = recept[s] * emid[s] + reads[h][UNIT:]


def join_kernel(
    n,
    nh,
    tp_ref,
    loc_ref,
    st_ref,
    r_ref,
    k_ref,
    v_ref,
    g_ref,
    rw_ref,
    gain_ref,
    bias_ref,
    skip_ref,
    w_hbm,
    out_ref,
    slabs,
    sbuf,
    sin,
    mixed,
    wbuf,
    near_out,
    near_in,
    far_out,
    far_in,
    acc,
    send1,
    recv1,
    send2,
    recv2,
    send3,
    recv3,
    send4,
    recv4,
    w_sem,
):
    me = lax.axis_index("seq")
    mh = lax.axis_index("head")
    hi, lo = mh // 2, mh % 2
    far = nh // 2
    channels, length = r_ref.shape
    units = channels // UNIT
    own = max(1, units // n)
    share = channels // n
    rows = out_ref.shape[0]

    w_copy = pltpu.make_async_copy(w_hbm, wbuf, w_sem)
    w_copy.start()

    barrier = pltpu.get_barrier_semaphore()
    for off in range(1, n):
        pl.semaphore_signal(barrier, inc=1, device_id={"seq": (me + off) % n}, device_id_type=MESH)
    for off in range(1, nh):
        pl.semaphore_signal(barrier, inc=1, device_id={"head": (mh + off) % nh}, device_id_type=MESH)
    pl.semaphore_wait(barrier, n - 1 + nh - 1)

    def first_row(d):
        return pl.multiple_of((d * share) // UNIT * UNIT, UNIT)

    sends = []
    for off in range(1, n):
        d = (me + off) % n
        copy = pltpu.make_async_remote_copy(
            src_ref=tp_ref.at[pl.ds(first_row(d), own * UNIT)],
            dst_ref=slabs.at[me],
            send_sem=send1.at[off],
            recv_sem=recv1.at[off],
            device_id={"seq": d},
            device_id_type=MESH,
        )
        copy.start()
        sends.append(copy)
    slabs[me] = tp_ref[pl.ds(first_row(me), own * UNIT), :]
    for copy in sends:
        copy.wait()

    state = [jnp.zeros((UNIT, UNIT), F32) for _ in range(own)]
    for j in range(n):
        for u in range(own):
            sbuf[j, u * UNIT : (u + 1) * UNIT, :] = state[u]
        if j + 1 < n:
            for u in range(own):
                item = slabs[j, u * UNIT : (u + 1) * UNIT, :]
                state[u] = mm(state[u], item[:, :UNIT]) + item[:, UNIT:]

    inner = pl.multiple_of((me * share) % UNIT, min(share, UNIT))
    mine = pl.ds(pl.multiple_of(me * share, share), share)
    sends = []
    for off in range(1, n):
        d = (me + off) % n
        copy = pltpu.make_async_remote_copy(
            src_ref=sbuf.at[d, pl.ds(inner, share)],
            dst_ref=sin.at[mine],
            send_sem=send2.at[off],
            recv_sem=recv2.at[off],
            device_id={"seq": d},
            device_id_type=MESH,
        )
        copy.start()
        sends.append(copy)
    sin[mine, :] = sbuf[me, pl.ds(inner, share), :]

    for copy in sends:
        copy.wait()

    def finish(p, carry):
        base = pl.multiple_of(p * 128, 128)
        rw = columns_of(rw_ref, p, 1)
        gain = columns_of(gain_ref, p, 1)
        bias = columns_of(bias_ref, p, 1)
        for u in range(2):
            s = pl.ds(base + u * UNIT, UNIT)
            c = slice(u * UNIT, (u + 1) * UNIT)
            y = loc_ref[s, :] + mm(sin[s, :], st_ref[s, :])
            y = y - jnp.mean(y, axis=0, keepdims=True)
            q = jnp.mean(y * y, axis=0, keepdims=True)
            normed = y * lax.rsqrt(q + 0.00064) * gain[c] + bias[c]
            rk = r_ref[s, :].astype(F32) * k_ref[s, :].astype(F32) * rw[c]
            bonus = jnp.sum(rk, axis=0, keepdims=True) * v_ref[s, :].astype(F32)
            mixed[s, :] = ((normed + bonus) * g_ref[s, :].astype(F32)).astype(BF16)
        return carry

    lax.fori_loop(0, units // 2, finish, 0)
    w_copy.wait()

    tile = 256

    def block(j, put):
        def body(i, carry):
            at = pl.multiple_of(i * tile, tile)
            wt = wbuf[pl.ds(pl.multiple_of(j * rows, rows) + at, tile), :]
            put(pl.ds(at, tile), jnp.dot(wt, mixed[...], preferred_element_type=F32))
            return carry

        lax.fori_loop(0, rows // tile, body, 0)

    near = []
    for f in range(far):
        h = (hi + 1 + f) % far

        def put(s, x, f=f):
            near_out[f, s, :] = x.astype(BF16)

        block(h * 2 + (1 - lo), put)
        copy = pltpu.make_async_remote_copy(
            src_ref=near_out.at[f],
            dst_ref=near_in.at[f],
            send_sem=send3.at[f],
            recv_sem=recv3.at[f],
            device_id={"head": hi * 2 + (1 - lo)},
            device_id_type=MESH,
        )
        copy.start()
        near.append(copy)
    away = []
    for f in range(far - 1):
        h = (hi + 1 + f) % far

        def put(s, x):
            acc[s, :] = x

        block(h * 2 + lo, put)
        near[f].wait()
        far_out[f] = (acc[...] + near_in[f].astype(F32)).astype(BF16)
        copy = pltpu.make_async_remote_copy(
            src_ref=far_out.at[f],
            dst_ref=far_in.at[f],
            send_sem=send4.at[f],
            recv_sem=recv4.at[f],
            device_id={"head": h * 2 + lo},
            device_id_type=MESH,
        )
        copy.start()
        away.append(copy)

    def put_last(s, x):
        acc[s, :] = x + skip_ref[s, :].astype(F32)

    block(mh, put_last)
    near[far - 1].wait()
    acc[...] += near_in[far - 1].astype(F32)
    for f in range(far - 1):
        away[f].wait()
        acc[...] += far_in[f].astype(F32)
    out_ref[...] = acc[...].astype(BF16)


def on_device(n, nh, skip, r, k, v, g, w, a, erasure, reward, gain, bias, weights):
    channels, length = r.shape
    rows = GROUP * UNIT
    flat = lambda x: x.reshape(channels // 128, 128)
    block = pl.BlockSpec((rows, length), lambda i: (i, 0))
    whole = pl.BlockSpec(memory_space=pltpu.VMEM)
    tp, loc, st = pl.pallas_call(
        local_kernel,
        grid=(channels // rows,),
        in_specs=[block] * 5 + [pl.BlockSpec((channels // 128, 128), lambda i: (0, 0))],
        out_specs=[pl.BlockSpec((rows, 2 * UNIT), lambda i: (i, 0)), block, block],
        out_shape=[
            jax.ShapeDtypeStruct((channels, 2 * UNIT), F32),
            jax.ShapeDtypeStruct((channels, length), F32),
            jax.ShapeDtypeStruct((channels, length), F32),
        ],
        compiler_params=pltpu.CompilerParams(vmem_limit_bytes=24 * 1024 * 1024),
        name="local",
    )(r, k, v, w, a, flat(erasure))
    own = max(1, channels // UNIT // n)
    out_rows = skip.shape[0]
    far = nh // 2
    dma = pltpu.SemaphoreType.DMA
    return pl.pallas_call(
        functools.partial(join_kernel, n, nh),
        out_shape=jax.ShapeDtypeStruct(skip.shape, BF16),
        in_specs=[whole] * 11 + [pl.BlockSpec(memory_space=pl.ANY)],
        out_specs=whole,
        scratch_shapes=[
            pltpu.VMEM((n, own * UNIT, 2 * UNIT), F32),
            pltpu.VMEM((n, own * UNIT, UNIT), F32),
            pltpu.VMEM((channels, UNIT), F32),
            pltpu.VMEM((channels, length), BF16),
            pltpu.VMEM(weights.shape, BF16),
            pltpu.VMEM((far, out_rows, length), BF16),
            pltpu.VMEM((far, out_rows, length), BF16),
            pltpu.VMEM((far, out_rows, length), BF16),
            pltpu.VMEM((far, out_rows, length), BF16),
            pltpu.VMEM((out_rows, length), F32),
            dma((n,)),
            dma((n,)),
            dma((n,)),
            dma((n,)),
            dma((far,)),
            dma((far,)),
            dma((far,)),
            dma((far,)),
            dma,
        ],
        compiler_params=pltpu.CompilerParams(
            collective_id=0, has_side_effects=True, vmem_limit_bytes=40 * 1024 * 1024
        ),
        name="join",
    )(tp, loc, st, r, k, v, g, flat(reward), flat(gain), flat(bias), skip, weights)


def solution(mesh):
    n, nh = mesh.shape["seq"], mesh.shape["head"]
    both, one = P("head", "seq"), P("head")
    return jax.shard_map(
        functools.partial(on_device, n, nh),
        mesh=mesh,
        in_specs=(both,) * 7 + (one,) * 4 + (P(None, "head"),),
        out_specs=both,
        check_vma=False,
    )
```

```python
import functools

import jax
import jax.numpy as jnp
from jax import lax
from jax.experimental import pallas as pl
from jax.experimental.pallas import tpu as pltpu
from jax.sharding import PartitionSpec as P

MESH = pl.DeviceIdType.MESH
UNIT = 64
GROUP = 4
F32 = jnp.float32
BF16 = jnp.bfloat16


def split(x):
    hi = x.astype(BF16)
    return hi, (x - hi.astype(F32)).astype(BF16)


def mm(a, b, ca=1, cb=0, passes=3):
    dims = (((ca,), (cb,)), ((), ()))
    if passes == 1:
        return lax.dot_general(a.astype(BF16), b.astype(BF16), dims, preferred_element_type=F32)
    if a.dtype == BF16:
        bh, bl = split(b)
        a2 = jnp.concatenate([a, a], axis=ca)
        b2 = jnp.concatenate([bh, bl], axis=cb)
        return lax.dot_general(a2, b2, dims, preferred_element_type=F32)
    ah, al = split(a)
    bh, bl = split(b)
    a3 = jnp.concatenate([ah, ah, al], axis=ca)
    b3 = jnp.concatenate([bh, bl, bh], axis=cb)
    return lax.dot_general(a3, b3, dims, preferred_element_type=F32)


def columns_of(row_ref, first, count):
    i = lax.broadcasted_iota(jnp.int32, (128, 128), 0)
    j = lax.broadcasted_iota(jnp.int32, (128, 128), 1)
    eye = i == j
    out = []
    for n in range(count):
        row = row_ref[pl.ds(first + n, 1), :]
        out.append(jnp.sum(jnp.where(eye, jnp.broadcast_to(row, (128, 128)), 0.0), axis=1, keepdims=True))
    return jnp.concatenate(out, axis=0) if count > 1 else out[0]


def local_group(p, r_ref, k_ref, v_ref, w_ref, a_ref, er_ref, tp_ref, loc_ref, st_ref):
    length = r_ref.shape[1]
    first = pl.multiple_of(p * (GROUP * UNIT), GROUP * UNIT)
    rows = pl.ds(first, GROUP * UNIT)
    mid_at = length // 2 - 1
    si = lax.broadcasted_iota(jnp.int32, (length, length), 0)
    ti = lax.broadcasted_iota(jnp.int32, (length, length), 1)
    ones = jnp.where(si <= ti, 1.0, 0.0) - jnp.where(si <= mid_at, 1.0, 0.0)
    w16 = w_ref[rows, :]
    c = jnp.dot(w16, ones.astype(BF16), preferred_element_type=F32)
    w = w16.astype(F32)
    er = columns_of(er_ref, p * (GROUP // 2), GROUP // 2)
    k = k_ref[rows, :].astype(F32)
    scaled = k * er
    heads = range(GROUP)
    sl = [slice(h * UNIT, (h + 1) * UNIT) for h in heads]
    kk = jnp.concatenate(
        [scaled[s] * lax.rsqrt(jnp.sum(scaled[s] * scaled[s], axis=0, keepdims=True) + 1e-06) for s in sl], axis=0
    )
    back = jnp.exp(-c)
    pulled_back = a_ref[rows, :].astype(F32) * kk * back
    keys_back = k * back
    removal = -kk * jnp.exp(c - w)
    recept = r_ref[rows, :].astype(F32) * jnp.exp(c)
    emid = jnp.exp(w[:, 0:1] - c[:, 0:1])
    eend = jnp.exp(c[:, length - 1 :])
    etot = emid * eend
    pulled_end = pulled_back * eend
    keys_end = keys_back * eend

    before = si < ti
    upto = si <= ti
    mix = [
        mm(
            jnp.concatenate([pulled_back[s], keys_back[s]], axis=1),
            jnp.concatenate([removal[s], recept[s]], axis=1),
            0,
            0,
        )
        for s in sl
    ]
    pair_mix = [jnp.where(before, m[:length, :length], 0.0) for m in mix]
    key_mix = [jnp.where(before, m[length:, :length], 0.0) for m in mix]
    pair_read = [jnp.where(upto, m[:length, length:], 0.0) for m in mix]
    key_read = [jnp.where(upto, m[length:, length:], 0.0) for m in mix]
    eye = jnp.where(si == ti, 1.0, 0.0)
    size = 1
    inv = None
    while size < length:
        joins = (si // (2 * size) == ti // (2 * size)) & (si // size != ti // size)
        off = [jnp.where(joins, m, 0.0) for m in pair_mix]
        if inv is None:
            inv = [eye + o for o in off]
        else:
            half = [mm(n, o) for n, o in zip(inv, off)]
            inv = [n + mm(x, n) for n, x in zip(inv, half)]
        size *= 2
    v16 = v_ref[rows, :]
    vk = [mm(v16[s], m) for s, m in zip(sl, key_mix)]
    solved = [mm(jnp.concatenate([x, removal[s]], axis=0), n) for x, s, n in zip(vk, sl, inv)]
    solved = [jnp.concatenate([x[:UNIT], x[UNIT:] * emid[s]], axis=0) for x, s in zip(solved, sl)]
    ends = [mm(x, pulled_end[s], 1, 1) for x, s in zip(solved, sl)]
    vke = [mm(v16[s], keys_end[s], 1, 1) for s in sl]
    reads = [mm(x, p) for x, p in zip(solved, pair_read)]
    vkr = [mm(v16[s], m) for s, m in zip(sl, key_read)]
    diag = lax.broadcasted_iota(jnp.int32, (UNIT, UNIT), 0) == lax.broadcasted_iota(jnp.int32, (UNIT, UNIT), 1)
    for h in heads:
        s = sl[h]
        d = pl.ds(first + h * UNIT, UNIT)
        trans = ends[h][UNIT:] + jnp.where(diag, jnp.broadcast_to(etot[s], (UNIT, UNIT)), 0.0)
        tp_ref[d, :] = jnp.concatenate([trans, ends[h][:UNIT] + vke[h]], axis=1)
        loc_ref[d, :] = reads[h][:UNIT] + vkr[h]
        st_ref[d, :] = recept[s] * emid[s] + reads[h][UNIT:]


def kernel(n, nh, *refs):
    names = INPUTS + ("out",) + SCRATCH
    join(n, nh, dict(zip(names, refs)))


INPUTS = ("r", "k", "v", "w", "a", "g", "er", "rw", "gain", "bias", "skip", "weights")
SCRATCH = tuple(x + "_v" for x in INPUTS) + (
    "tp", "loc", "st", "bonus", "slabs", "sbuf", "sin", "mixed",
    "near_out", "near_in", "far_out", "far_in", "acc",
    "send1", "recv1", "send2", "recv2", "send3", "recv3", "send4", "recv4", "load",
)
CHUNKS = 4


def join(n, nh, ref):
    me = lax.axis_index("seq")
    mh = lax.axis_index("head")
    hi, lo = mh // 2, mh % 2
    far = nh // 2
    here = {x: ref[x + "_v"] for x in INPUTS}
    channels, length = here["r"].shape
    units = channels // UNIT
    own = max(1, units // n)
    share = channels // n
    part = min(share, UNIT)
    rows = ref["out"].shape[0]
    slabs, sbuf, sin, mixed, acc = (ref[x] for x in ("slabs", "sbuf", "sin", "mixed", "acc"))
    tp, loc, st, bonus = (ref[x] for x in ("tp", "loc", "st", "bonus"))

    order = ("er", "k", "w", "a", "r", "v", "rw", "gain", "bias", "g", "skip", "weights")
    loads = {}
    for i, x in enumerate(order):
        loads[x] = pltpu.make_async_copy(ref[x], here[x], ref["load"].at[i])
        loads[x].start()

    barrier = pltpu.get_barrier_semaphore()
    for off in range(1, n):
        pl.semaphore_signal(barrier, inc=1, device_id={"seq": (me + off) % n}, device_id_type=MESH)
    for off in range(1, nh):
        pl.semaphore_signal(barrier, inc=1, device_id={"head": (mh + off) % nh}, device_id_type=MESH)
    for x in order[:6]:
        loads[x].wait()
    pl.semaphore_wait(barrier, n - 1 + nh - 1)

    def state_copy(d):
        off = (d - me + n) % n
        row = pl.multiple_of((d * share) // UNIT * UNIT, UNIT)
        return pltpu.make_async_remote_copy(
            src_ref=tp.at[pl.ds(row, own * UNIT)],
            dst_ref=slabs.at[me],
            send_sem=ref["send1"].at[off],
            recv_sem=ref["recv1"].at[off],
            device_id={"seq": d},
            device_id_type=MESH,
        )

    groups = units // GROUP
    owners = GROUP * UNIT // share

    def local_step(i, carry):
        p = (me // owners + 1 + i) % groups
        local_group(p, *(here[x] for x in ("r", "k", "v", "w", "a", "er")), tp, loc, st)
        for q in range(owners):
            d = p * owners + q

            @pl.when(d != me)
            def _():
                state_copy(d).start()

        return carry

    lax.fori_loop(0, groups, local_step, 0)
    slabs[me] = tp[pl.ds(pl.multiple_of((me * share) // UNIT * UNIT, UNIT), own * UNIT), :]

    for x in order[6:11]:
        loads[x].wait()

    def bonus_step(p, carry):
        base = pl.multiple_of(p * 128, 128)
        rw = columns_of(here["rw"], p, 1)
        for u in range(2):
            s = pl.ds(base + u * UNIT, UNIT)
            rk = here["r"][s, :].astype(F32) * here["k"][s, :].astype(F32) * rw[u * UNIT : (u + 1) * UNIT]
            bonus[s, :] = jnp.sum(rk, axis=0, keepdims=True) * here["v"][s, :].astype(F32)
        return carry

    lax.fori_loop(0, units // 2, bonus_step, 0)
    for off in range(1, n):
        state_copy((me + off) % n).wait()

    state = [jnp.zeros((UNIT, UNIT), F32) for _ in range(own)]
    for j in range(n):
        sbuf[j] = jnp.concatenate(state, axis=1).astype(sbuf.dtype)
        if j + 1 < n:
            for u in range(own):
                item = slabs[j, u * UNIT : (u + 1) * UNIT, :]
                state[u] = mm(state[u], item[:, :UNIT]) + item[:, UNIT:]

    inner = pl.multiple_of((me * share) % UNIT, part)
    mine = pl.ds(pl.multiple_of(me * part, part), part)
    sends = []
    for off in range(1, n):
        d = (me + off) % n
        copy = pltpu.make_async_remote_copy(
            src_ref=sbuf.at[d, pl.ds(inner, part)],
            dst_ref=sin.at[mine],
            send_sem=ref["send2"].at[off],
            recv_sem=ref["recv2"].at[off],
            device_id={"seq": d},
            device_id_type=MESH,
        )
        copy.start()
        sends.append(copy)
    sin[mine, :] = sbuf[me, pl.ds(inner, part), :]
    for copy in sends:
        copy.wait()

    def finish(p, carry):
        base = pl.multiple_of(p * 128, 128)
        gain = columns_of(here["gain"], p, 1)
        bias = columns_of(here["bias"], p, 1)
        for u in range(2):
            s = pl.ds(base + u * UNIT, UNIT)
            c = slice(u * UNIT, (u + 1) * UNIT)
            if own == 1:
                arriving = sin[s, :]
            else:
                arriving = sin[pl.ds(pl.multiple_of(p * 2 // own * UNIT, UNIT), UNIT), u % own * UNIT : (u % own + 1) * UNIT]
            y = loc[s, :] + mm(arriving, st[s, :])
            y = y - jnp.mean(y, axis=0, keepdims=True)
            q = jnp.mean(y * y, axis=0, keepdims=True)
            normed = y * lax.rsqrt(q + 0.00064) * gain[c] + bias[c]
            mixed[s, :] = ((normed + bonus[s, :]) * here["g"][s, :].astype(F32)).astype(BF16)
        return carry

    lax.fori_loop(0, units // 2, finish, 0)
    loads["weights"].wait()

    tile = rows // CHUNKS

    def piece(j, c):
        at = pl.multiple_of(j * rows, rows) + c * tile
        return jnp.dot(here["weights"][pl.ds(at, tile), :], mixed[...], preferred_element_type=F32)

    def near_copy(f, c):
        s = pl.ds(c * tile, tile)
        return pltpu.make_async_remote_copy(
            src_ref=ref["near_out"].at[f, s],
            dst_ref=ref["near_in"].at[f, s],
            send_sem=ref["send3"].at[f, c],
            recv_sem=ref["recv3"].at[f, c],
            device_id={"head": hi * 2 + (1 - lo)},
            device_id_type=MESH,
        )

    def far_copy(f, c):
        s = pl.ds(c * tile, tile)
        return pltpu.make_async_remote_copy(
            src_ref=ref["far_out"].at[f, s],
            dst_ref=ref["far_in"].at[f, s],
            send_sem=ref["send4"].at[f, c],
            recv_sem=ref["recv4"].at[f, c],
            device_id={"head": (hi + 1 + f) % far * 2 + lo},
            device_id_type=MESH,
        )

    def near_all(f):
        for c in range(CHUNKS):
            h = (hi + 1 + f) % far
            ref["near_out"][f, c * tile : (c + 1) * tile, :] = piece(h * 2 + (1 - lo), c).astype(BF16)
            near_copy(f, c).start()

    near_all(0)
    for f in range(far - 1):
        for c in range(CHUNKS):
            s = slice(c * tile, (c + 1) * tile)
            x = piece((hi + 1 + f) % far * 2 + lo, c)
            near_copy(f, c).wait()
            ref["far_out"][f, s, :] = (x + ref["near_in"][f, s, :].astype(F32)).astype(BF16)
            far_copy(f, c).start()
        near_all(f + 1)
    for c in range(CHUNKS):
        s = slice(c * tile, (c + 1) * tile)
        x = piece(mh, c) + here["skip"][s, :].astype(F32)
        near_copy(far - 1, c).wait()
        acc[s, :] = x + ref["near_in"][far - 1, s, :].astype(F32)
    for c in range(CHUNKS):
        s = slice(c * tile, (c + 1) * tile)
        x = acc[s, :]
        for f in range(far - 1):
            far_copy(f, c).wait()
            x = x + ref["far_in"][f, s, :].astype(F32)
        ref["out"][s, :] = x.astype(BF16)


def on_device(n, nh, skip, r, k, v, g, w, a, erasure, reward, gain, bias, weights):
    channels, length = r.shape
    flat = lambda x: x.reshape(channels // 128, 128)
    own = max(1, channels // UNIT // n)
    part = min(channels // n, UNIT)
    rows = skip.shape[0]
    far = nh // 2
    dma = pltpu.SemaphoreType.DMA
    operands = (r, k, v, w, a, g, flat(erasure), flat(reward), flat(gain), flat(bias), skip, weights)
    return pl.pallas_call(
        functools.partial(kernel, n, nh),
        out_shape=jax.ShapeDtypeStruct(skip.shape, BF16),
        in_specs=[pl.BlockSpec(memory_space=pl.ANY)] * len(operands),
        out_specs=pl.BlockSpec(memory_space=pltpu.VMEM),
        scratch_shapes=[pltpu.VMEM(x.shape, x.dtype) for x in operands]
        + [
            pltpu.VMEM((channels, 2 * UNIT), F32),
            pltpu.VMEM((channels, length), F32),
            pltpu.VMEM((channels, length), F32),
            pltpu.VMEM((channels, length), F32),
            pltpu.VMEM((n, own * UNIT, 2 * UNIT), F32),
            pltpu.VMEM((n, UNIT, own * UNIT), F32),
            pltpu.VMEM((n * part, own * UNIT), F32),
            pltpu.VMEM((channels, length), BF16),
            pltpu.VMEM((far, rows, length), BF16),
            pltpu.VMEM((far, rows, length), BF16),
            pltpu.VMEM((far, rows, length), BF16),
            pltpu.VMEM((far, rows, length), BF16),
            pltpu.VMEM((rows, length), F32),
            dma((n,)),
            dma((n,)),
            dma((n,)),
            dma((n,)),
            dma((far, CHUNKS)),
            dma((far, CHUNKS)),
            dma((far, CHUNKS)),
            dma((far, CHUNKS)),
            dma((len(operands),)),
        ],
        compiler_params=pltpu.CompilerParams(
            collective_id=0, has_side_effects=True, vmem_limit_bytes=62 * 1024 * 1024
        ),
        name="timemix",
    )(*operands)


def solution(mesh):
    n, nh = mesh.shape["seq"], mesh.shape["head"]
    both, one = P("head", "seq"), P("head")
    return jax.shard_map(
        functools.partial(on_device, n, nh),
        mesh=mesh,
        in_specs=(both,) * 7 + (one,) * 4 + (P(None, "head"),),
        out_specs=both,
        check_vma=False,
    )
```

```python
import functools

import jax
import jax.numpy as jnp
from jax import lax
from jax.experimental import pallas as pl
from jax.experimental.pallas import tpu as pltpu
from jax.sharding import PartitionSpec as P

MESH = pl.DeviceIdType.MESH
UNIT = 64
GROUP = 4
F32 = jnp.float32
BF16 = jnp.bfloat16


def split(x):
    hi = x.astype(BF16)
    return hi, (x - hi.astype(F32)).astype(BF16)


def mm(a, b, ca=1, cb=0, passes=3):
    dims = (((ca,), (cb,)), ((), ()))
    if passes == 1:
        return lax.dot_general(a.astype(BF16), b.astype(BF16), dims, preferred_element_type=F32)
    if a.dtype == BF16:
        bh, bl = split(b)
        a2 = jnp.concatenate([a, a], axis=ca)
        b2 = jnp.concatenate([bh, bl], axis=cb)
        return lax.dot_general(a2, b2, dims, preferred_element_type=F32)
    ah, al = split(a)
    bh, bl = split(b)
    a3 = jnp.concatenate([ah, ah, al], axis=ca)
    b3 = jnp.concatenate([bh, bl, bh], axis=cb)
    return lax.dot_general(a3, b3, dims, preferred_element_type=F32)


def columns_of(row_ref, first, count):
    i = lax.broadcasted_iota(jnp.int32, (128, 128), 0)
    j = lax.broadcasted_iota(jnp.int32, (128, 128), 1)
    eye = i == j
    out = []
    for n in range(count):
        row = row_ref[pl.ds(first + n, 1), :]
        out.append(jnp.sum(jnp.where(eye, jnp.broadcast_to(row, (128, 128)), 0.0), axis=1, keepdims=True))
    return jnp.concatenate(out, axis=0) if count > 1 else out[0]


def local_group(p, r_ref, k_ref, v_ref, w_ref, a_ref, er_ref, tp_ref, loc_ref, st_ref):
    length = r_ref.shape[1]
    first = pl.multiple_of(p * (GROUP * UNIT), GROUP * UNIT)
    rows = pl.ds(first, GROUP * UNIT)
    mid_at = length // 2 - 1
    si = lax.broadcasted_iota(jnp.int32, (length, length), 0)
    ti = lax.broadcasted_iota(jnp.int32, (length, length), 1)
    ones = jnp.where(si <= ti, 1.0, 0.0) - jnp.where(si <= mid_at, 1.0, 0.0)
    w16 = w_ref[rows, :]
    c = jnp.dot(w16, ones.astype(BF16), preferred_element_type=F32)
    w = w16.astype(F32)
    er = columns_of(er_ref, p * (GROUP // 2), GROUP // 2)
    k = k_ref[rows, :].astype(F32)
    scaled = k * er
    heads = range(GROUP)
    sl = [slice(h * UNIT, (h + 1) * UNIT) for h in heads]
    kk = jnp.concatenate(
        [scaled[s] * lax.rsqrt(jnp.sum(scaled[s] * scaled[s], axis=0, keepdims=True) + 1e-06) for s in sl], axis=0
    )
    back = jnp.exp(-c)
    pulled_back = a_ref[rows, :].astype(F32) * kk * back
    keys_back = k * back
    removal = -kk * jnp.exp(c - w)
    recept = r_ref[rows, :].astype(F32) * jnp.exp(c)
    emid = jnp.exp(w[:, 0:1] - c[:, 0:1])
    eend = jnp.exp(c[:, length - 1 :])
    etot = emid * eend
    pulled_end = pulled_back * eend
    keys_end = keys_back * eend

    before = si < ti
    upto = si <= ti
    mix = [
        mm(
            jnp.concatenate([pulled_back[s], keys_back[s]], axis=1),
            jnp.concatenate([removal[s], recept[s]], axis=1),
            0,
            0,
        )
        for s in sl
    ]
    pair_mix = [jnp.where(before, m[:length, :length], 0.0) for m in mix]
    key_mix = [jnp.where(before, m[length:, :length], 0.0) for m in mix]
    pair_read = [jnp.where(upto, m[:length, length:], 0.0) for m in mix]
    key_read = [jnp.where(upto, m[length:, length:], 0.0) for m in mix]
    eye = jnp.where(si == ti, 1.0, 0.0)
    size = 1
    inv = None
    while size < length:
        joins = (si // (2 * size) == ti // (2 * size)) & (si // size != ti // size)
        off = [jnp.where(joins, m, 0.0) for m in pair_mix]
        if inv is None:
            inv = [eye + o for o in off]
        else:
            half = [mm(n, o, passes=1) for n, o in zip(inv, off)]
            inv = [n + mm(x, n, passes=1) for n, x in zip(inv, half)]
        size *= 2
    v16 = v_ref[rows, :]
    vk = [mm(v16[s], m) for s, m in zip(sl, key_mix)]
    solved = [mm(jnp.concatenate([x, removal[s]], axis=0), n) for x, s, n in zip(vk, sl, inv)]
    solved = [jnp.concatenate([x[:UNIT], x[UNIT:] * emid[s]], axis=0) for x, s in zip(solved, sl)]
    ends = [mm(x, pulled_end[s], 1, 1) for x, s in zip(solved, sl)]
    vke = [mm(v16[s], keys_end[s], 1, 1) for s in sl]
    reads = [mm(x, p) for x, p in zip(solved, pair_read)]
    vkr = [mm(v16[s], m) for s, m in zip(sl, key_read)]
    diag = lax.broadcasted_iota(jnp.int32, (UNIT, UNIT), 0) == lax.broadcasted_iota(jnp.int32, (UNIT, UNIT), 1)
    for h in heads:
        s = sl[h]
        d = pl.ds(first + h * UNIT, UNIT)
        trans = ends[h][UNIT:] + jnp.where(diag, jnp.broadcast_to(etot[s], (UNIT, UNIT)), 0.0)
        tp_ref[d, :] = jnp.concatenate([trans, ends[h][:UNIT] + vke[h]], axis=1).astype(BF16)
        loc_ref[d, :] = reads[h][:UNIT] + vkr[h]
        st_ref[d, :] = recept[s] * emid[s] + reads[h][UNIT:]


def kernel(n, nh, *refs):
    names = INPUTS + ("out",) + SCRATCH
    join(n, nh, dict(zip(names, refs)))


INPUTS = ("r", "k", "v", "w", "a", "g", "er", "rw", "gain", "bias", "skip", "weights")
SCRATCH = tuple(x + "_v" for x in INPUTS) + (
    "tp", "loc", "st", "bonus", "slabs", "sbuf", "sin", "mixed",
    "near_out", "near_in", "far_out", "far_in", "acc",
    "send1", "recv1", "send2", "recv2", "send3", "recv3", "send4", "recv4", "load",
)
CHUNKS = 4


def join(n, nh, ref):
    me = lax.axis_index("seq")
    mh = lax.axis_index("head")
    hi, lo = mh // 2, mh % 2
    far = nh // 2
    here = {x: ref[x + "_v"] for x in INPUTS}
    channels, length = here["r"].shape
    units = channels // UNIT
    own = max(1, units // n)
    share = channels // n
    part = min(share, UNIT)
    rows = ref["out"].shape[0]
    slabs, sbuf, sin, mixed, acc = (ref[x] for x in ("slabs", "sbuf", "sin", "mixed", "acc"))
    tp, loc, st, bonus = (ref[x] for x in ("tp", "loc", "st", "bonus"))

    order = ("er", "k", "w", "a", "r", "v", "rw", "gain", "bias", "g", "skip", "weights")
    loads = {}
    for i, x in enumerate(order):
        loads[x] = pltpu.make_async_copy(ref[x], here[x], ref["load"].at[i])
        loads[x].start()

    barrier = pltpu.get_barrier_semaphore()
    for off in range(1, n):
        pl.semaphore_signal(barrier, inc=1, device_id={"seq": (me + off) % n}, device_id_type=MESH)
    for off in range(1, nh):
        pl.semaphore_signal(barrier, inc=1, device_id={"head": (mh + off) % nh}, device_id_type=MESH)
    for x in order[:6]:
        loads[x].wait()

    def state_copy(d):
        off = (d - me + n) % n
        row = pl.multiple_of((d * share) // UNIT * UNIT, UNIT)
        return pltpu.make_async_remote_copy(
            src_ref=tp.at[pl.ds(row, own * UNIT)],
            dst_ref=slabs.at[me],
            send_sem=ref["send1"].at[off],
            recv_sem=ref["recv1"].at[off],
            device_id={"seq": d},
            device_id_type=MESH,
        )

    groups = units // GROUP
    owners = GROUP * UNIT // share

    def local_step(i, carry):
        p = (me // owners + 1 + i) % groups
        local_group(p, *(here[x] for x in ("r", "k", "v", "w", "a", "er")), tp, loc, st)
        if carry is None:
            pl.semaphore_wait(barrier, n - 1 + nh - 1)
        for q in range(owners):
            d = p * owners + q

            @pl.when(d != me)
            def _():
                state_copy(d).start()

        return carry

    local_step(0, None)
    lax.fori_loop(1, groups, local_step, 0)
    slabs[me] = tp[pl.ds(pl.multiple_of((me * share) // UNIT * UNIT, UNIT), own * UNIT), :]

    for x in order[6:11]:
        loads[x].wait()

    def bonus_step(p, carry):
        base = pl.multiple_of(p * 128, 128)
        rw = columns_of(here["rw"], p, 1)
        for u in range(2):
            s = pl.ds(base + u * UNIT, UNIT)
            rk = here["r"][s, :].astype(F32) * here["k"][s, :].astype(F32) * rw[u * UNIT : (u + 1) * UNIT]
            bonus[s, :] = jnp.sum(rk, axis=0, keepdims=True) * here["v"][s, :].astype(F32)
        return carry

    lax.fori_loop(0, units // 2, bonus_step, 0)
    for off in range(1, n):
        state_copy((me + off) % n).wait()

    state = [jnp.zeros((UNIT, UNIT), F32) for _ in range(own)]
    for j in range(n):
        sbuf[j] = jnp.concatenate(state, axis=1).astype(sbuf.dtype)
        if j + 1 < n:
            for u in range(own):
                item = slabs[j, u * UNIT : (u + 1) * UNIT, :].astype(F32)
                state[u] = mm(state[u], item[:, :UNIT]) + item[:, UNIT:]

    inner = pl.multiple_of((me * share) % UNIT, part)
    mine = pl.ds(pl.multiple_of(me * part, part), part)
    sends = []
    for off in range(1, n):
        d = (me + off) % n
        copy = pltpu.make_async_remote_copy(
            src_ref=sbuf.at[d, pl.ds(inner, part)],
            dst_ref=sin.at[mine],
            send_sem=ref["send2"].at[off],
            recv_sem=ref["recv2"].at[off],
            device_id={"seq": d},
            device_id_type=MESH,
        )
        copy.start()
        sends.append(copy)
    sin[mine, :] = sbuf[me, pl.ds(inner, part), :]
    for copy in sends:
        copy.wait()

    def finish(p, carry):
        base = pl.multiple_of(p * 128, 128)
        gain = columns_of(here["gain"], p, 1)
        bias = columns_of(here["bias"], p, 1)
        for u in range(2):
            s = pl.ds(base + u * UNIT, UNIT)
            c = slice(u * UNIT, (u + 1) * UNIT)
            if own == 1:
                arriving = sin[s, :]
            else:
                arriving = sin[pl.ds(pl.multiple_of(p * 2 // own * UNIT, UNIT), UNIT), u % own * UNIT : (u % own + 1) * UNIT]
            y = loc[s, :] + mm(arriving, st[s, :])
            y = y - jnp.mean(y, axis=0, keepdims=True)
            q = jnp.mean(y * y, axis=0, keepdims=True)
            normed = y * lax.rsqrt(q + 0.00064) * gain[c] + bias[c]
            mixed[s, :] = ((normed + bonus[s, :]) * here["g"][s, :].astype(F32)).astype(BF16)
        return carry

    lax.fori_loop(0, units // 2, finish, 0)
    loads["weights"].wait()

    tile = rows // CHUNKS

    def piece(j, c):
        at = pl.multiple_of(j * rows, rows) + c * tile
        return jnp.dot(here["weights"][pl.ds(at, tile), :], mixed[...], preferred_element_type=F32)

    def near_copy(f, c):
        s = pl.ds(c * tile, tile)
        return pltpu.make_async_remote_copy(
            src_ref=ref["near_out"].at[f, s],
            dst_ref=ref["near_in"].at[f, s],
            send_sem=ref["send3"].at[f, c],
            recv_sem=ref["recv3"].at[f, c],
            device_id={"head": hi * 2 + (1 - lo)},
            device_id_type=MESH,
        )

    def far_copy(f, c):
        s = pl.ds(c * tile, tile)
        return pltpu.make_async_remote_copy(
            src_ref=ref["far_out"].at[f, s],
            dst_ref=ref["far_in"].at[f, s],
            send_sem=ref["send4"].at[f, c],
            recv_sem=ref["recv4"].at[f, c],
            device_id={"head": (hi + 1 + f) % far * 2 + lo},
            device_id_type=MESH,
        )

    def near_all(f):
        for c in range(CHUNKS):
            h = (hi + 1 + f) % far
            ref["near_out"][f, c * tile : (c + 1) * tile, :] = piece(h * 2 + (1 - lo), c).astype(BF16)
            near_copy(f, c).start()

    near_all(0)
    for f in range(far - 1):
        for c in range(CHUNKS):
            s = slice(c * tile, (c + 1) * tile)
            x = piece((hi + 1 + f) % far * 2 + lo, c)
            near_copy(f, c).wait()
            ref["far_out"][f, s, :] = (x + ref["near_in"][f, s, :].astype(F32)).astype(BF16)
            far_copy(f, c).start()
        near_all(f + 1)
    for c in range(CHUNKS):
        s = slice(c * tile, (c + 1) * tile)
        x = piece(mh, c) + here["skip"][s, :].astype(F32)
        near_copy(far - 1, c).wait()
        acc[s, :] = x + ref["near_in"][far - 1, s, :].astype(F32)
    for c in range(CHUNKS):
        s = slice(c * tile, (c + 1) * tile)
        x = acc[s, :]
        for f in range(far - 1):
            far_copy(f, c).wait()
            x = x + ref["far_in"][f, s, :].astype(F32)
        ref["out"][s, :] = x.astype(BF16)


def on_device(n, nh, skip, r, k, v, g, w, a, erasure, reward, gain, bias, weights):
    channels, length = r.shape
    flat = lambda x: x.reshape(channels // 128, 128)
    own = max(1, channels // UNIT // n)
    part = min(channels // n, UNIT)
    rows = skip.shape[0]
    far = nh // 2
    dma = pltpu.SemaphoreType.DMA
    operands = (r, k, v, w, a, g, flat(erasure), flat(reward), flat(gain), flat(bias), skip, weights)
    return pl.pallas_call(
        functools.partial(kernel, n, nh),
        out_shape=jax.ShapeDtypeStruct(skip.shape, BF16),
        in_specs=[pl.BlockSpec(memory_space=pl.ANY)] * len(operands),
        out_specs=pl.BlockSpec(memory_space=pltpu.VMEM),
        scratch_shapes=[pltpu.VMEM(x.shape, x.dtype) for x in operands]
        + [
            pltpu.VMEM((channels, 2 * UNIT), BF16),
            pltpu.VMEM((channels, length), F32),
            pltpu.VMEM((channels, length), F32),
            pltpu.VMEM((channels, length), F32),
            pltpu.VMEM((n, own * UNIT, 2 * UNIT), BF16),
            pltpu.VMEM((n, UNIT, own * UNIT), BF16),
            pltpu.VMEM((n * part, own * UNIT), BF16),
            pltpu.VMEM((channels, length), BF16),
            pltpu.VMEM((far, rows, length), BF16),
            pltpu.VMEM((far, rows, length), BF16),
            pltpu.VMEM((far, rows, length), BF16),
            pltpu.VMEM((far, rows, length), BF16),
            pltpu.VMEM((rows, length), F32),
            dma((n,)),
            dma((n,)),
            dma((n,)),
            dma((n,)),
            dma((far, CHUNKS)),
            dma((far, CHUNKS)),
            dma((far, CHUNKS)),
            dma((far, CHUNKS)),
            dma((len(operands),)),
        ],
        compiler_params=pltpu.CompilerParams(
            collective_id=0, has_side_effects=True, vmem_limit_bytes=62 * 1024 * 1024
        ),
        name="timemix",
    )(*operands)


def solution(mesh):
    n, nh = mesh.shape["seq"], mesh.shape["head"]
    both, one = P("head", "seq"), P("head")
    return jax.shard_map(
        functools.partial(on_device, n, nh),
        mesh=mesh,
        in_specs=(both,) * 7 + (one,) * 4 + (P(None, "head"),),
        out_specs=both,
        check_vma=False,
    )
```
